1024 devices in a mesh: blk: 64 (over y, x), section: 16 (over z, core).
Axes of the slice: x: 8, y: 8, z: 8, core: 2. Of those that a mesh axis runs over, the one named last changes fastest.
Arguments:
- stream_sent: bfloat16 [16, 256, 3072], P('section', 'blk'), may hold values from -6 to 6
- grad_sent: bfloat16 [16, 256, 3072], P('section', 'blk'), may hold values from -3 to 3
- preact_now: bfloat16 [16, 256, 16384], P('section', None, 'blk'), may hold values from -16 to 16
- preact_back: bfloat16 [16, 256, 16384], P('section', None, 'blk'), may hold values from -6 to 6
- down_weight: bfloat16 [16, 16384, 3072], P('section', 'blk'), may hold values from -0.109375 to 0.109375
- block_mask: int32 [16, 128, 24], P('section', 'blk'), may hold values from 0 to 1, as said below
Outputs:
- stream_out: bfloat16 [16, 256, 3072], P('section', 'blk')
- preact_grad: bfloat16 [16, 256, 16384], P('section', None, 'blk')
- weight_grad: bfloat16 [16, 16384, 3072], P('section', 'blk')
The draws below stay inside these ranges and needn't reach their ends.
Inputs may be any that keep to these rules, and one draw needn't show every extreme that they name: `block_mask`: 1 marks a nonzero 128 x 128 block of the down projection, 0 an empty one.
All inputs are finite; a program needn't handle non-finite values.
Results may differ from the reference program's by a relative error of at most 0.005.
Values may be sent and summed in bfloat16 or wider, within the bound.
A program may use at most 32 MiB of HBM per device.

```python
import jax
import jax.numpy as jnp
from jax import lax

D = 3072
FF = 16384
BLOCK = 128
SECTIONS = 16
TOKENS = 256


def draw_block_mask(key, part):
    first_key, second_key = jax.random.split(jax.random.fold_in(key, 7))
    share = jax.random.randint(first_key, (SECTIONS, FF // BLOCK, 1), 3, 30)
    drawn = jax.random.randint(second_key, (SECTIONS, FF // BLOCK, D // BLOCK), 0, 32)
    return (drawn < share).astype(jnp.int32)


def spiked(array, own_key, source, target, blocks, factor):
    owner, partner = [(jnp.arange(array.shape[axis_at]) // (array.shape[axis_at] // blocks)).reshape([-1 if axis == axis_at else 1 for axis in range(array.ndim)]) for axis_at in (source, target)]
    chosen = jax.random.permutation(own_key, blocks)[partner]
    strong = (owner == chosen) | (owner == (partner + blocks // 2) % blocks)
    return jnp.where(strong, factor * array, array)


def shard_levels(key, dims, cuts, smallest, largest):
    def one(position, shards_of):
        draws = jax.random.uniform(jax.random.fold_in(jax.random.fold_in(key, 6), position), (shards_of,), jnp.float32, smallest / len(cuts), largest / len(cuts))
        return jnp.repeat(jnp.exp(draws), dims[position] // shards_of).reshape((-1,) + (1,) * (len(dims) - position - 1))

    gain = one(*cuts[0])
    for cut in cuts[1:]:
        gain = gain * one(*cut)
    return gain


def normal_values(key, extent, spread, most, cuts=(), held_as=jnp.bfloat16):
    array = jax.random.normal(key, extent, jnp.float32) * spread
    if len(cuts) > 0:
        array = shard_levels(key, extent, cuts, -0.22, 0.18) * array
    return jnp.clip(array, min=-most, max=most).astype(held_as)


def noise_with(stream_key, extent, width, reach, cuts, heavy, held_as=jnp.bfloat16):
    values = width * jax.random.normal(stream_key, extent, jnp.float32)
    if cuts:
        values = values * shard_levels(stream_key, extent, cuts, -0.22, 0.18)
    return jnp.clip(spiked(values, jax.random.fold_in(stream_key, 3), *heavy), -reach, reach).astype(held_as)


def setup_inputs(seed: int = 0) -> dict:
    arg_keys = jax.random.split(jax.random.key(seed), 7)
    stream_sent = normal_values(arg_keys[0], (SECTIONS, TOKENS, D), 1.0, 6.0, ((0, 16), (1, 64)))
    grad_sent = normal_values(arg_keys[1], (SECTIONS, TOKENS, D), 0.5, 3.0, ((0, 16), (1, 64)))
    preact_now = noise_with(arg_keys[2], (SECTIONS, TOKENS, FF), 1.0, 16.0, ((0, 16), (2, 64)), (2, 1, 64, 4.0))
    preact_back = normal_values(arg_keys[3], (SECTIONS, TOKENS, FF), 1.0, 6.0, ((0, 16), (2, 64)))
    down_weight = normal_values(arg_keys[4], (SECTIONS, FF, D), D ** -0.5, 0.109375, ((0, 16), (1, 64)))
    block_mask = draw_block_mask(jax.random.fold_in(arg_keys[6], 71), 0)
    return {"stream_sent": stream_sent, "grad_sent": grad_sent, "preact_now": preact_now, "preact_back": preact_back, "down_weight": down_weight, "block_mask": block_mask}


def expand(blocks):
    values = blocks.astype(jnp.bfloat16)
    return jnp.repeat(jnp.repeat(values, BLOCK, axis=0), BLOCK, axis=1)

def one_section(pieces):
    stream, grad, preact_a, preact_b, weight, blocks = pieces
    expanded = expand(blocks)
    masked = weight * expanded
    hidden_now = jax.nn.gelu(preact_a.astype(jnp.float32)).astype(jnp.bfloat16)
    summed = jnp.dot(hidden_now, masked, preferred_element_type=jnp.float32)
    stream_out = (stream.astype(jnp.float32) + summed).astype(jnp.bfloat16)
    grad_hidden = lax.dot_general(grad, masked, (((1,), (1,)), ((), ())), preferred_element_type=jnp.float32)
    preact_f = preact_b.astype(jnp.float32)
    hidden_f, pullback = jax.vjp(jax.nn.gelu, preact_f)
    preact_grad = pullback(grad_hidden)[0].astype(jnp.bfloat16)
    hidden_back = hidden_f.astype(jnp.bfloat16)
    weight_full = lax.dot_general(hidden_back, grad, (((0,), (0,)), ((), ())), preferred_element_type=jnp.float32)
    weight_grad = (weight_full * expanded.astype(jnp.float32)).astype(jnp.bfloat16)
    return (stream_out, preact_grad, weight_grad)

def reference(stream_sent, grad_sent, preact_now, preact_back, down_weight, block_mask):
    stream = jnp.concatenate([stream_sent[:1], stream_sent[:-1]], axis=0)
    grad = jnp.concatenate([grad_sent[1:], grad_sent[-1:]], axis=0)
    stream_out, preact_grad, weight_grad = lax.map(one_section, (stream, grad, preact_now, preact_back, down_weight, block_mask))
    return (stream_out, preact_grad, weight_grad)
```

```python
import functools
import math

import jax
import jax.numpy as jnp
from jax import lax
from jax.experimental import pallas as pl
from jax.experimental.pallas import tpu as pltpu
from jax.sharding import PartitionSpec as P

BLOCK = 128
SUBS = 2
MESH = pl.DeviceIdType.MESH
GELU_C = math.sqrt(2.0 / math.pi)
GELU_A = 0.044715
F32 = jnp.float32
BF16 = jnp.bfloat16


def gelu(v):
    return v * (0.5 * (1.0 + jnp.tanh(GELU_C * (v + GELU_A * (v * v * v)))))


def gelu_and_slope(v):
    squared = v * v
    t = jnp.tanh(GELU_C * (v + GELU_A * (squared * v)))
    share = 0.5 * (1.0 + t)
    slope = share + v * (0.5 * (1.0 - t * t) * (GELU_C * (1.0 + 3.0 * GELU_A * squared)))
    return v * share, slope


def dot(a, b):
    return jnp.dot(a, b, preferred_element_type=F32)


def kernel(
    n, sections, stream_ref, grad_ref, now_ref, back_ref, w_ref, mask_ref,
    out_ref, pg_ref, wg_ref,
    mask_s, w_v, now_v, back_v, own_grad, own_stream, part32, part16, hop_in, hop_out, pieces, gathered,
    fan_out, fan_in, slope_v, hidden_t, gh_v, out_v, pg_v, wg_v,
    load_sem, hop_send, hop_recv, ring_send, ring_recv, piece_send, piece_recv, fan_send, fan_recv, relay_sem, store_sem,
):
    hidden, width = w_v.shape
    half = width // 2
    sub = half // SUBS
    tokens = gathered.shape[1]
    mine = own_grad.shape[0]
    rows = n * mine
    reach = n // 2
    blk = lax.axis_index("blk")
    section = lax.axis_index("section")
    place = (lax.rem(blk, n), lax.div(blk, n))

    def wrap(v):
        return lax.rem(v + 2 * n, n)

    def device(axis, at, where):
        index = place[1] * n + at if axis == 0 else at * n + place[0]
        return {"blk": index, "section": where}

    def half_columns(h):
        return pl.ds(h * half, half)

    def sub_columns(c):
        return pl.ds(c * sub, sub)

    def block_rows(b):
        return pl.ds(pl.multiple_of(b * rows, rows), rows)

    barrier = pltpu.get_barrier_semaphore()
    for offset in range(1, n):
        for axis in range(2):
            at = wrap(place[axis] + offset)
            pl.semaphore_signal(barrier, inc=1, device_id=device(axis, at, section), device_id_type=MESH)

    @pl.when(section < sections - 1)
    def _():
        pl.semaphore_signal(barrier, inc=1, device_id=device(0, place[0], section + 1), device_id_type=MESH)
        for offset in range(1, n):
            for axis in range(2):
                at = wrap(place[axis] + offset)
                pl.semaphore_signal(barrier, inc=1, device_id=device(axis, at, section + 1), device_id_type=MESH)

    @pl.when(section > 0)
    def _():
        pl.semaphore_signal(barrier, inc=1, device_id=device(0, place[0], section - 1), device_id_type=MESH)

    loads = [
        pltpu.make_async_copy(now_ref.at[0], now_v, load_sem.at[0]),
        pltpu.make_async_copy(mask_ref.at[0], mask_s, load_sem.at[1]),
        pltpu.make_async_copy(grad_ref.at[0], own_grad, load_sem.at[2]),
        pltpu.make_async_copy(back_ref.at[0], back_v, load_sem.at[3]),
    ]
    w_loads = []
    for chunk in range(2 * SUBS):
        columns = pl.ds(chunk * sub, sub)
        w_loads.append(pltpu.make_async_copy(w_ref.at[0, :, columns], w_v.at[:, columns], load_sem.at[4 + chunk]))
    for copy in loads[:2] + w_loads + loads[2:]:
        copy.start()

    def mask_tile(i, j):
        return jnp.full((BLOCK, BLOCK), mask_s[i, j].astype(F32), F32)

    to_row = lax.broadcasted_iota(jnp.int32, (tokens, tokens), 0)
    from_row = lax.broadcasted_iota(jnp.int32, (tokens, tokens), 1)
    shift_rows, shift_mine = rows.bit_length() - 1, mine.bit_length() - 1
    wanted = (
        ((to_row & (rows - 1)) >> shift_mine) * rows + (to_row >> shift_rows) * mine + (to_row & (mine - 1))
    )
    permute = jnp.where(from_row == wanted, 1.0, 0.0).astype(BF16)

    loads[0].wait()
    hidden_now = gelu(now_v[...].astype(F32)).astype(BF16)
    hidden_half = (dot(permute, hidden_now).astype(BF16), hidden_now)
    loads[1].wait()
    for chunk in range(2 * SUBS):
        w_loads[chunk].wait()
        for j in range(chunk * sub // BLOCK, (chunk + 1) * sub // BLOCK):
            for i in range(hidden // BLOCK):
                tile = (pl.ds(i * BLOCK, BLOCK), pl.ds(j * BLOCK, BLOCK))
                w_v[tile] = w_v[tile] * mask_tile(i, j).astype(BF16)
        h, c = divmod(chunk, SUBS)
        product = dot(hidden_half[h], w_v[:, chunk * sub : (chunk + 1) * sub])
        part32[h, :, c * sub : (c + 1) * sub] = product
        part16[h, :, c * sub : (c + 1) * sub] = product.astype(BF16)
    loads[2].wait()

    first, last = section == 0, section == sections - 1
    expected = 2 * (n - 1) + jnp.where(first, 0, 2 * n - 1) + jnp.where(last, 0, 1)
    pl.semaphore_wait(barrier, expected)

    def piece_copy(h, offset, where, slot):
        return pltpu.make_async_remote_copy(
            src_ref=own_grad.at[:, half_columns(h)],
            dst_ref=pieces.at[h, place[h]],
            send_sem=piece_send.at[slot, h, offset],
            recv_sem=piece_recv.at[h, place[h]],
            device_id=device(h, wrap(place[h] + offset), where),
            device_id_type=MESH,
        )

    order = sorted(range(1, n), key=lambda offset: -min(offset, n - offset))
    before = jnp.maximum(section - 1, 0)
    after = jnp.minimum(section + 1, sections - 1)

    @pl.when(section > 0)
    def _():
        for offset in order + [0]:
            for h in range(2):
                piece_copy(h, offset, before, 0).start()

    own_pieces = [
        pltpu.make_async_copy(own_grad.at[:, half_columns(h)], pieces.at[h, place[h]], relay_sem.at[2 + h])
        for h in range(2)
    ]

    @pl.when(last)
    def _():
        for offset in order:
            for h in range(2):
                piece_copy(h, offset, section, 1).start()
        for copy in own_pieces:
            copy.start()

    steps_of = lambda c, way: reach if (c + way) % 2 == 0 else reach - 1
    chains = [(h, c, way) for c in range(SUBS) for h in range(2) for way in range(2)]

    def hop_copy(h, c, way, step):
        turn = 1 - 2 * way
        target = wrap(place[h] + turn * (steps_of(c, way) - step + 1))
        if step == 1:
            source = part16.at[h, block_rows(target), sub_columns(c)]
        else:
            source = hop_out.at[h, way, step - 2, :, sub_columns(c)]
        return pltpu.make_async_remote_copy(
            src_ref=source,
            dst_ref=hop_in.at[h, way, step - 1, :, sub_columns(c)],
            send_sem=hop_send.at[h, c, way, step - 1],
            recv_sem=hop_recv.at[h, c, way, step - 1],
            device_id=device(h, wrap(place[h] + turn), section),
            device_id_type=MESH,
        )

    for h, c, way in chains:
        if steps_of(c, way) >= 1:
            hop_copy(h, c, way, 1).start()

    relay_copy = pltpu.make_async_remote_copy(
        src_ref=stream_ref.at[0],
        dst_ref=own_stream,
        send_sem=relay_sem.at[0],
        recv_sem=relay_sem.at[1],
        device_id=device(0, place[0], after),
        device_id_type=MESH,
    )
    stream_copy = pltpu.make_async_copy(stream_ref.at[0], own_stream, relay_sem.at[4])

    @pl.when(section < sections - 1)
    def _():
        relay_copy.start()

    @pl.when(first)
    def _():
        stream_copy.start()

    loads[3].wait()
    hidden_back, slope = gelu_and_slope(back_v[...].astype(F32))
    slope_v[...] = slope
    transposed = jnp.transpose(hidden_back).astype(BF16)
    hidden_t[0] = transposed
    hidden_t[1] = dot(transposed, permute).astype(BF16)

    def ring_copy(h, c, way, step):
        turn = 1 - 2 * way
        region = gathered.at[h, block_rows(wrap(place[1 - h] - turn * (step - 1))), sub_columns(c)]
        return pltpu.make_async_remote_copy(
            src_ref=region,
            dst_ref=region,
            send_sem=ring_send.at[h, c, way, step - 1],
            recv_sem=ring_recv.at[h, c, way, step - 1],
            device_id=device(1 - h, wrap(place[1 - h] + turn), section),
            device_id_type=MESH,
        )

    def ring_arrival(h, c, way, step):
        turn = 1 - 2 * way
        region = gathered.at[h, block_rows(wrap(place[1 - h] - turn * step)), sub_columns(c)]
        return pltpu.make_async_remote_copy(
            src_ref=region,
            dst_ref=region,
            send_sem=ring_send.at[h, c, way, step - 1],
            recv_sem=ring_recv.at[h, c, way, step - 1],
            device_id=device(1 - h, wrap(place[1 - h] + turn), section),
            device_id_type=MESH,
        )

    def piece_arrival(h, at):
        return pltpu.make_async_remote_copy(
            src_ref=own_grad.at[:, half_columns(h)],
            dst_ref=pieces.at[h, at],
            send_sem=piece_send.at[0, h, 0],
            recv_sem=piece_recv.at[h, at],
            device_id=device(0, place[0], after),
            device_id_type=MESH,
        )

    @pl.when(last)
    def _():
        for copy in own_pieces:
            copy.wait()

    @pl.when(section < sections - 1)
    def _():
        for h in range(2):
            piece_arrival(h, place[h]).wait_recv()

    for h in range(2):
        for offset in range(1, n):
            piece_arrival(h, wrap(place[h] + offset)).wait_recv()
        block = jnp.concatenate([pieces[h, at].astype(F32) for at in range(n)], axis=0)
        gathered[h, block_rows(place[1 - h]), :] = block.astype(BF16)
        for c in range(SUBS):
            for way in range(2):
                if steps_of(c, way) >= 1:
                    ring_copy(h, c, way, 1).start()

    for step in range(2, reach + 1):
        for h, c, way in chains:
            if steps_of(c, way) >= step:
                turn = 1 - 2 * way
                hop_copy(h, c, way, step - 1).wait_recv()
                target = wrap(place[h] + turn * (steps_of(c, way) - step + 1))
                cols = slice(c * sub, (c + 1) * sub)
                total = hop_in[h, way, step - 2, :, cols].astype(F32) + part32[h, block_rows(target), cols]
                hop_out[h, way, step - 2, :, cols] = total.astype(BF16)
                hop_copy(h, c, way, step).start()
        for h, c, way in chains:
            if steps_of(c, way) >= step:
                ring_arrival(h, c, way, step - 1).wait_recv()
                ring_copy(h, c, way, step).start()

    def fan_copy(h, offset):
        at = wrap(place[1 - h] + offset)
        return pltpu.make_async_remote_copy(
            src_ref=fan_out.at[h, at],
            dst_ref=fan_in.at[h, place[1 - h]],
            send_sem=fan_send.at[h, offset],
            recv_sem=fan_recv.at[h, place[1 - h]],
            device_id=device(1 - h, at, section),
            device_id_type=MESH,
        )

    for h in range(2):
        for c in range(SUBS):
            cols = slice(c * sub, (c + 1) * sub)
            total = part32[h, block_rows(place[h]), cols]
            for way in range(2):
                if steps_of(c, way) >= 1:
                    hop_copy(h, c, way, steps_of(c, way)).wait_recv()
                    total = total + hop_in[h, way, steps_of(c, way) - 1, :, cols].astype(F32)
            for at in range(n):
                fan_out[h, at, :, cols] = total[at * mine : (at + 1) * mine, :]
        for offset in order:
            fan_copy(h, offset).start()

    for h, c, way in chains:
        if steps_of(c, way) >= 1:
            ring_arrival(h, c, way, steps_of(c, way)).wait_recv()

    contract_last = (((1,), (1,)), ((), ()))
    gh_v[1] = lax.dot_general(gathered[1], w_v[:, half:], contract_last, preferred_element_type=F32)
    gh_v[0] = lax.dot_general(gathered[0], w_v[:, :half], contract_last, preferred_element_type=F32)
    pack = 16 // mine
    for group in range(tokens // 16):
        found = []
        for part in range(pack):
            along_y, along_x = divmod(group * pack + part, n)
            found.append(gh_v[1, pl.ds(along_x * rows + along_y * mine, mine), :])
        here = pl.ds(group * 16, 16)
        pg_v[here, :] = ((gh_v[0, here, :] + jnp.concatenate(found, axis=0)) * slope_v[here, :]).astype(BF16)
    stores = [pltpu.make_async_copy(pg_v, pg_ref.at[0], store_sem.at[0])]
    stores[0].start()
    for chunk in range(2 * SUBS):
        h, c = divmod(chunk, SUBS)
        product = dot(hidden_t[h], gathered[h, :, c * sub : (c + 1) * sub])
        for j in range(sub // BLOCK):
            for i in range(hidden // BLOCK):
                column = chunk * sub // BLOCK + j
                tile = product[i * BLOCK : (i + 1) * BLOCK, j * BLOCK : (j + 1) * BLOCK] * mask_tile(i, column)
                wg_v[pl.ds(i * BLOCK, BLOCK), pl.ds(column * BLOCK, BLOCK)] = tile.astype(BF16)
        columns = pl.ds(chunk * sub, sub)
        stores.append(pltpu.make_async_copy(wg_v.at[:, columns], wg_ref.at[0, :, columns], store_sem.at[1 + chunk]))
        stores[-1].start()

    @pl.when(section < sections - 1)
    def _():
        relay_copy.wait_send()

    @pl.when(section > 0)
    def _():
        relay_copy.wait_recv()

    @pl.when(first)
    def _():
        stream_copy.wait()

    for h in range(2):
        for offset in range(1, n):
            at = wrap(place[1 - h] + offset)
            pltpu.make_async_remote_copy(
                src_ref=fan_out.at[h, at],
                dst_ref=fan_in.at[h, at],
                send_sem=fan_send.at[h, offset],
                recv_sem=fan_recv.at[h, at],
                device_id=device(1 - h, at, section),
                device_id_type=MESH,
            ).wait_recv()
        total = own_stream[:, h * half : (h + 1) * half].astype(F32) + fan_out[h, place[1 - h]]
        for offset in range(1, n):
            total = total + fan_in[h, wrap(place[1 - h] + offset)]
        out_v[:, h * half : (h + 1) * half] = total.astype(BF16)
    stores.append(pltpu.make_async_copy(out_v, out_ref.at[0], store_sem.at[1 + 2 * SUBS]))
    stores[-1].start()

    @pl.when(section > 0)
    def _():
        for offset in range(n):
            for h in range(2):
                piece_copy(h, offset, before, 0).wait_send()

    @pl.when(last)
    def _():
        for offset in range(1, n):
            for h in range(2):
                piece_copy(h, offset, section, 1).wait_send()

    for h, c, way in chains:
        for step in range(1, steps_of(c, way) + 1):
            hop_copy(h, c, way, step).wait_send()
            ring_copy(h, c, way, step).wait_send()
    for h in range(2):
        for offset in range(1, n):
            fan_copy(h, offset).wait_send()
    for copy in stores:
        copy.wait()


def body(n, sections, stream_sent, grad_sent, preact_now, preact_back, down_weight, block_mask):
    mine, width = stream_sent.shape[1:]
    tokens, hidden = preact_now.shape[1:]
    half = width // 2
    rows, reach = n * mine, n // 2
    anywhere = pl.BlockSpec(memory_space=pl.ANY)
    dma = pltpu.SemaphoreType.DMA
    return pl.pallas_call(
        functools.partial(kernel, n, sections),
        name="relay_layer",
        out_shape=(
            jax.ShapeDtypeStruct(stream_sent.shape, BF16),
            jax.ShapeDtypeStruct(preact_back.shape, BF16),
            jax.ShapeDtypeStruct(down_weight.shape, BF16),
        ),
        in_specs=[anywhere] * 6,
        out_specs=(anywhere,) * 3,
        scratch_shapes=[
            pltpu.SMEM(block_mask.shape[1:], jnp.int32),
            pltpu.VMEM((hidden, width), BF16),
            pltpu.VMEM((tokens, hidden), BF16),
            pltpu.VMEM((tokens, hidden), BF16),
            pltpu.VMEM((mine, width), BF16),
            pltpu.VMEM((mine, width), BF16),
            pltpu.VMEM((2, tokens, half), F32),
            pltpu.VMEM((2, tokens, half), BF16),
            pltpu.VMEM((2, 2, reach, rows, half), BF16),
            pltpu.VMEM((2, 2, reach - 1, rows, half), BF16),
            pltpu.VMEM((2, n, mine, half), BF16),
            pltpu.VMEM((2, tokens, half), BF16),
            pltpu.VMEM((2, n, mine, half), F32),
            pltpu.VMEM((2, n, mine, half), F32),
            pltpu.VMEM((tokens, hidden), F32),
            pltpu.VMEM((2, hidden, tokens), BF16),
            pltpu.VMEM((2, tokens, hidden), F32),
            pltpu.VMEM((mine, width), BF16),
            pltpu.VMEM((tokens, hidden), BF16),
            pltpu.VMEM((hidden, width), BF16),
            dma((4 + 2 * SUBS,)),
            dma((2, SUBS, 2, reach)),
            dma((2, SUBS, 2, reach)),
            dma((2, SUBS, 2, reach)),
            dma((2, SUBS, 2, reach)),
            dma((2, 2, n)),
            dma((2, n)),
            dma((2, n)),
            dma((2, n)),
            dma((5,)),
            dma((2 + 2 * SUBS,)),
        ],
        compiler_params=pltpu.CompilerParams(collective_id=0, has_side_effects=True),
    )(stream_sent, grad_sent, preact_now, preact_back, down_weight, block_mask)


def solution(mesh):
    n = math.isqrt(mesh.shape["blk"])
    placed = (
        P("section", "blk", None),
        P("section", "blk", None),
        P("section", None, "blk"),
        P("section", None, "blk"),
        P("section", "blk", None),
        P("section", "blk", None),
    )
    return jax.shard_map(
        functools.partial(body, n, mesh.shape["section"]),
        mesh=mesh,
        in_specs=placed,
        out_specs=(P("section", "blk", None), P("section", None, "blk"), P("section", "blk", None)),
        check_vma=False,
    )
```

```python
import functools
import math

import jax
import jax.numpy as jnp
from jax import lax
from jax.experimental import pallas as pl
from jax.experimental.pallas import tpu as pltpu
from jax.sharding import PartitionSpec as P

BLOCK = 128
SUBS = 2
MESH = pl.DeviceIdType.MESH
GELU_C = math.sqrt(2.0 / math.pi)
GELU_A = 0.044715
F32 = jnp.float32
BF16 = jnp.bfloat16


def gelu(v):
    return v * (0.5 * (1.0 + jnp.tanh(GELU_C * (v + GELU_A * (v * v * v)))))


def gelu_and_slope(v):
    squared = v * v
    t = jnp.tanh(GELU_C * (v + GELU_A * (squared * v)))
    share = 0.5 * (1.0 + t)
    slope = share + v * (0.5 * (1.0 - t * t) * (GELU_C * (1.0 + 3.0 * GELU_A * squared)))
    return v * share, slope


def dot(a, b):
    return jnp.dot(a, b, preferred_element_type=F32)


def kernel(
    n, sections, stream_ref, grad_ref, now_ref, back_ref, w_ref, mask_ref,
    out_v, pg_v, wg_v,
    mask_s, w_v, now_v, back_v, own_grad, own_stream, part32, part16, hop_in, hop_out, pieces, gathered,
    fan_out, fan_in, total_v, slope_v, hidden_t, gh_v,
    load_sem, hop_recv, ring_send, ring_recv, piece_send, piece_recv, fan_recv, relay_sem,
):
    hidden, width = w_v.shape
    half = width // 2
    sub = half // SUBS
    tokens = gathered.shape[1]
    mine = own_grad.shape[0]
    rows = n * mine
    reach = n // 2
    blk = lax.axis_index("blk")
    section = lax.axis_index("section")
    place = (lax.rem(blk, n), lax.div(blk, n))

    def wrap(v):
        return lax.rem(v + 2 * n, n)

    def device(axis, at, where):
        index = place[1] * n + at if axis == 0 else at * n + place[0]
        return {"blk": index, "section": where}

    def half_columns(h):
        return pl.ds(h * half, half)

    def sub_columns(c):
        return pl.ds(c * sub, sub)

    def block_rows(b):
        return pl.ds(pl.multiple_of(b * rows, rows), rows)

    loads = [
        pltpu.make_async_copy(now_ref.at[0], now_v, load_sem.at[0]),
        pltpu.make_async_copy(mask_ref.at[0], mask_s, load_sem.at[1]),
        pltpu.make_async_copy(grad_ref.at[0], own_grad, load_sem.at[2]),
        pltpu.make_async_copy(back_ref.at[0], back_v, load_sem.at[3]),
    ]
    w_loads = []
    for chunk in range(2 * SUBS):
        columns = pl.ds(chunk * sub, sub)
        w_loads.append(pltpu.make_async_copy(w_ref.at[0, :, columns], w_v.at[:, columns], load_sem.at[4 + chunk]))
    for copy in loads[:2] + w_loads + loads[2:]:
        copy.start()

    barrier = pltpu.get_barrier_semaphore()
    order = sorted(range(1, n), key=lambda offset: -min(offset, n - offset))
    for offset in order:
        for axis in range(2):
            at = wrap(place[axis] + offset)
            pl.semaphore_signal(barrier, inc=1, device_id=device(axis, at, section), device_id_type=MESH)

    @pl.when(section < sections - 1)
    def _():
        pl.semaphore_signal(barrier, inc=1, device_id=device(0, place[0], section + 1), device_id_type=MESH)
        for offset in order:
            for axis in range(2):
                at = wrap(place[axis] + offset)
                pl.semaphore_signal(barrier, inc=1, device_id=device(axis, at, section + 1), device_id_type=MESH)

    @pl.when(section > 0)
    def _():
        pl.semaphore_signal(barrier, inc=1, device_id=device(0, place[0], section - 1), device_id_type=MESH)

    def mask_tile(i, j):
        return jnp.full((BLOCK, BLOCK), mask_s[i, j].astype(F32), F32)

    to_row = lax.broadcasted_iota(jnp.int32, (tokens, tokens), 0)
    from_row = lax.broadcasted_iota(jnp.int32, (tokens, tokens), 1)
    shift_rows, shift_mine = rows.bit_length() - 1, mine.bit_length() - 1
    wanted = (
        ((to_row & (rows - 1)) >> shift_mine) * rows + (to_row >> shift_rows) * mine + (to_row & (mine - 1))
    )
    permute = jnp.where(from_row == wanted, 1.0, 0.0).astype(BF16)

    loads[0].wait()
    hidden_now = gelu(now_v[...].astype(F32)).astype(BF16)
    hidden_half = (dot(permute, hidden_now).astype(BF16), hidden_now)
    loads[1].wait()
    for chunk in range(2 * SUBS):
        w_loads[chunk].wait()
        for j in range(chunk * sub // BLOCK, (chunk + 1) * sub // BLOCK):
            for i in range(hidden // BLOCK):
                tile = (pl.ds(i * BLOCK, BLOCK), pl.ds(j * BLOCK, BLOCK))
                w_v[tile] = w_v[tile] * mask_tile(i, j).astype(BF16)
        h, c = divmod(chunk, SUBS)
        product = dot(hidden_half[h], w_v[:, chunk * sub : (chunk + 1) * sub])
        part32[h, :, c * sub : (c + 1) * sub] = product
        part16[h, :, c * sub : (c + 1) * sub] = product.astype(BF16)
    loads[2].wait()

    first, last = section == 0, section == sections - 1
    expected = 2 * (n - 1) + jnp.where(first, 0, 2 * n - 1) + jnp.where(last, 0, 1)
    pl.semaphore_wait(barrier, expected)

    def piece_copy(h, offset, where, slot):
        return pltpu.make_async_remote_copy(
            src_ref=own_grad.at[:, half_columns(h)],
            dst_ref=pieces.at[h, place[h]],
            send_sem=piece_send.at[slot],
            recv_sem=piece_recv.at[h],
            device_id=device(h, wrap(place[h] + offset), where),
            device_id_type=MESH,
        )

    before = jnp.maximum(section - 1, 0)
    after = jnp.minimum(section + 1, sections - 1)

    @pl.when(section > 0)
    def _():
        for offset in order + [0]:
            for h in range(2):
                piece_copy(h, offset, before, 0).start()

    own_pieces = [
        pltpu.make_async_copy(own_grad.at[:, half_columns(h)], pieces.at[h, place[h]], relay_sem.at[2 + h])
        for h in range(2)
    ]

    @pl.when(last)
    def _():
        for offset in order:
            for h in range(2):
                piece_copy(h, offset, section, 1).start()
        for copy in own_pieces:
            copy.start()

    steps_of = lambda c, way: reach if (c + way) % 2 == 0 else reach - 1
    chains = [(h, c, way) for c in range(SUBS) for h in range(2) for way in range(2)]

    def hop_copy(h, c, way, step):
        turn = 1 - 2 * way
        target = wrap(place[h] + turn * (steps_of(c, way) - step + 1))
        if step == 1:
            source = part16.at[h, block_rows(target), sub_columns(c)]
        else:
            source = hop_out.at[h, way, step - 2, :, sub_columns(c)]
        return pltpu.make_async_remote_copy(
            src_ref=source,
            dst_ref=hop_in.at[h, way, step - 1, :, sub_columns(c)],
            send_sem=ring_send.at[0],
            recv_sem=hop_recv.at[h, c, way, step - 1],
            device_id=device(h, wrap(place[h] + turn), section),
            device_id_type=MESH,
        )

    for h, c, way in chains:
        if steps_of(c, way) >= 1:
            hop_copy(h, c, way, 1).start()

    relay_copy = pltpu.make_async_remote_copy(
        src_ref=stream_ref.at[0],
        dst_ref=own_stream,
        send_sem=relay_sem.at[0],
        recv_sem=relay_sem.at[1],
        device_id=device(0, place[0], after),
        device_id_type=MESH,
    )
    stream_copy = pltpu.make_async_copy(stream_ref.at[0], own_stream, relay_sem.at[4])

    @pl.when(section < sections - 1)
    def _():
        relay_copy.start()

    @pl.when(first)
    def _():
        stream_copy.start()

    loads[3].wait()
    hidden_back, slope = gelu_and_slope(back_v[...].astype(F32))
    slope_v[...] = slope
    transposed = jnp.transpose(hidden_back).astype(BF16)
    hidden_t[0] = transposed
    hidden_t[1] = dot(transposed, permute).astype(BF16)

    def ring_copy(h, c, way, step):
        turn = 1 - 2 * way
        region = gathered.at[h, block_rows(wrap(place[1 - h] - turn * (step - 1))), sub_columns(c)]
        return pltpu.make_async_remote_copy(
            src_ref=region,
            dst_ref=region,
            send_sem=ring_send.at[1],
            recv_sem=ring_recv.at[h, c, way, step - 1],
            device_id=device(1 - h, wrap(place[1 - h] + turn), section),
            device_id_type=MESH,
        )

    def ring_arrival(h, c, way, step):
        turn = 1 - 2 * way
        region = gathered.at[h, block_rows(wrap(place[1 - h] - turn * step)), sub_columns(c)]
        return pltpu.make_async_remote_copy(
            src_ref=region,
            dst_ref=region,
            send_sem=ring_send.at[1],
            recv_sem=ring_recv.at[h, c, way, step - 1],
            device_id=device(1 - h, wrap(place[1 - h] + turn), section),
            device_id_type=MESH,
        )

    def waiter(region, sem):
        return pltpu.make_async_remote_copy(
            src_ref=region,
            dst_ref=region,
            send_sem=sem,
            recv_sem=sem,
            device_id=device(0, place[0], after),
            device_id_type=MESH,
        )

    def hop_onward(h, c, way, step):
        turn = 1 - 2 * way
        hop_copy(h, c, way, step - 1).wait_recv()
        target = wrap(place[h] + turn * (steps_of(c, way) - step + 1))
        cols = slice(c * sub, (c + 1) * sub)
        total = hop_in[h, way, step - 2, :, cols].astype(F32) + part32[h, block_rows(target), cols]
        hop_out[h, way, step - 2, :, cols] = total.astype(BF16)
        hop_copy(h, c, way, step).start()

    def ring_onward(h, c, way, step):
        ring_arrival(h, c, way, step - 1).wait_recv()
        ring_copy(h, c, way, step).start()

    def start_ring():
        @pl.when(last)
        def _():
            for h in range(2):
                own_pieces[h].wait()
                waiter(pieces.at[h, pl.ds(0, n - 1)], piece_recv.at[h]).wait_recv()

        @pl.when(section < sections - 1)
        def _():
            for h in range(2):
                waiter(pieces.at[h], piece_recv.at[h]).wait_recv()

        for h in range(2):
            block = jnp.concatenate([pieces[h, at].astype(F32) for at in range(n)], axis=0)
            gathered[h, block_rows(place[1 - h]), :] = block.astype(BF16)
        for h, c, way in chains:
            if steps_of(c, way) >= 1:
                ring_copy(h, c, way, 1).start()

    for step in range(2, reach + 1):
        for c in range(SUBS):
            for chain in chains:
                if chain[1] == c and steps_of(*chain[1:]) >= step:
                    hop_onward(*chain, step)
            if step > 2:
                for chain in chains:
                    if chain[1] == c and steps_of(*chain[1:]) >= step - 1:
                        ring_onward(*chain, step - 1)
        if step == 2:
            start_ring()

    def fan_copy(h, offset):
        at = wrap(place[1 - h] + offset)
        return pltpu.make_async_remote_copy(
            src_ref=fan_out.at[h, at],
            dst_ref=fan_in.at[h, place[1 - h]],
            send_sem=ring_send.at[2],
            recv_sem=fan_recv.at[h],
            device_id=device(1 - h, at, section),
            device_id_type=MESH,
        )

    for h in range(2):
        for c in range(SUBS):
            cols = slice(c * sub, (c + 1) * sub)
            total = part32[h, block_rows(place[h]), cols]
            for way in range(2):
                if steps_of(c, way) >= 1:
                    hop_copy(h, c, way, steps_of(c, way)).wait_recv()
                    total = total + hop_in[h, way, steps_of(c, way) - 1, :, cols].astype(F32)
            for at in range(n):
                total_v[h, at, :, cols] = total[at * mine : (at + 1) * mine, :]
                fan_out[h, at, :, cols] = total[at * mine : (at + 1) * mine, :].astype(BF16)
        for offset in order:
            fan_copy(h, offset).start()

    for chain in chains:
        if steps_of(*chain[1:]) >= reach:
            ring_onward(*chain, reach)

    contract_last = (((1,), (1,)), ((), ()))
    for c in range(SUBS):
        for h in range(2):
            for way in range(2):
                if steps_of(c, way) >= 1:
                    ring_arrival(h, c, way, steps_of(c, way)).wait_recv()
            arrived = gathered[h, :, c * sub : (c + 1) * sub]
            start = h * half + c * sub
            product = lax.dot_general(
                arrived, w_v[:, start : start + sub], contract_last, preferred_element_type=F32
            )
            gh_v[h] = product if c == 0 else gh_v[h] + product
            product = dot(hidden_t[h], arrived)
            for j in range(sub // BLOCK):
                for i in range(hidden // BLOCK):
                    column = start // BLOCK + j
                    tile = product[i * BLOCK : (i + 1) * BLOCK, j * BLOCK : (j + 1) * BLOCK] * mask_tile(i, column)
                    wg_v[pl.ds(i * BLOCK, BLOCK), pl.ds(column * BLOCK, BLOCK)] = tile.astype(BF16)
    pack = 16 // mine
    for group in range(tokens // 16):
        found = []
        for part in range(pack):
            along_y, along_x = divmod(group * pack + part, n)
            found.append(gh_v[1, pl.ds(along_x * rows + along_y * mine, mine), :])
        here = pl.ds(group * 16, 16)
        pg_v[here, :] = ((gh_v[0, here, :] + jnp.concatenate(found, axis=0)) * slope_v[here, :]).astype(BF16)

    @pl.when(section < sections - 1)
    def _():
        relay_copy.wait_send()

    @pl.when(section > 0)
    def _():
        relay_copy.wait_recv()

    @pl.when(first)
    def _():
        stream_copy.wait()

    for h in range(2):
        waiter(fan_in.at[h, pl.ds(0, n - 1)], fan_recv.at[h]).wait_recv()
        total = own_stream[:, h * half : (h + 1) * half].astype(F32) + total_v[h, place[1 - h]]
        for offset in range(1, n):
            total = total + fan_in[h, wrap(place[1 - h] + offset)].astype(F32)
        out_v[:, h * half : (h + 1) * half] = total.astype(BF16)

    @pl.when(section > 0)
    def _():
        for h in range(2):
            waiter(pieces.at[h], piece_send.at[0]).wait_send()

    @pl.when(last)
    def _():
        for h in range(2):
            waiter(pieces.at[h, pl.ds(0, n - 1)], piece_send.at[1]).wait_send()

    for h in range(2):
        waiter(gathered.at[h, pl.ds(0, (n - 1) * rows)], ring_send.at[0]).wait_send()
        waiter(gathered.at[h, pl.ds(0, (n - 1) * rows)], ring_send.at[1]).wait_send()
        waiter(fan_in.at[h, pl.ds(0, n - 1)], ring_send.at[2]).wait_send()


def store_kernel(*refs):
    copies = [pltpu.make_async_copy(refs[k], refs[3 + k].at[0], refs[6].at[k]) for k in range(3)]
    for copy in copies:
        copy.start()
    for copy in copies:
        copy.wait()


def body(n, sections, stream_sent, grad_sent, preact_now, preact_back, down_weight, block_mask):
    mine, width = stream_sent.shape[1:]
    tokens, hidden = preact_now.shape[1:]
    half = width // 2
    rows, reach = n * mine, n // 2
    anywhere = pl.BlockSpec(memory_space=pl.ANY)
    dma = pltpu.SemaphoreType.DMA
    held = pl.pallas_call(
        functools.partial(kernel, n, sections),
        name="relay_layer",
        out_shape=(
            pltpu.VMEM((mine, width), BF16),
            pltpu.VMEM((tokens, hidden), BF16),
            pltpu.VMEM((hidden, width), BF16),
        ),
        in_specs=[anywhere] * 6,
        out_specs=(pl.BlockSpec(memory_space=pltpu.VMEM),) * 3,
        scratch_shapes=[
            pltpu.SMEM(block_mask.shape[1:], jnp.int32),
            pltpu.VMEM((hidden, width), BF16),
            pltpu.VMEM((tokens, hidden), BF16),
            pltpu.VMEM((tokens, hidden), BF16),
            pltpu.VMEM((mine, width), BF16),
            pltpu.VMEM((mine, width), BF16),
            pltpu.VMEM((2, tokens, half), F32),
            pltpu.VMEM((2, tokens, half), BF16),
            pltpu.VMEM((2, 2, reach, rows, half), BF16),
            pltpu.VMEM((2, 2, reach - 1, rows, half), BF16),
            pltpu.VMEM((2, n, mine, half), BF16),
            pltpu.VMEM((2, tokens, half), BF16),
            pltpu.VMEM((2, n, mine, half), BF16),
            pltpu.VMEM((2, n, mine, half), BF16),
            pltpu.VMEM((2, n, mine, half), F32),
            pltpu.VMEM((tokens, hidden), F32),
            pltpu.VMEM((2, hidden, tokens), BF16),
            pltpu.VMEM((2, tokens, hidden), F32),
            dma((4 + 2 * SUBS,)),
            dma((2, SUBS, 2, reach)),
            dma((3,)),
            dma((2, SUBS, 2, reach)),
            dma((2,)),
            dma((2,)),
            dma((2,)),
            dma((5,)),
        ],
        compiler_params=pltpu.CompilerParams(collective_id=0, has_side_effects=True),
    )(stream_sent, grad_sent, preact_now, preact_back, down_weight, block_mask)
    return pl.pallas_call(
        store_kernel,
        name="store_outputs",
        out_shape=(
            jax.ShapeDtypeStruct(stream_sent.shape, BF16),
            jax.ShapeDtypeStruct(preact_back.shape, BF16),
            jax.ShapeDtypeStruct(down_weight.shape, BF16),
        ),
        in_specs=[pl.BlockSpec(memory_space=pltpu.VMEM)] * 3,
        out_specs=(anywhere,) * 3,
        scratch_shapes=[dma((3,))],
    )(*[pltpu.with_memory_space_constraint(a, pltpu.VMEM) for a in held])


def solution(mesh):
    n = math.isqrt(mesh.shape["blk"])
    placed = (
        P("section", "blk", None),
        P("section", "blk", None),
        P("section", None, "blk"),
        P("section", None, "blk"),
        P("section", "blk", None),
        P("section", "blk", None),
    )
    return jax.shard_map(
        functools.partial(body, n, mesh.shape["section"]),
        mesh=mesh,
        in_specs=placed,
        out_specs=(P("section", "blk", None), P("section", None, "blk"), P("section", "blk", None)),
        check_vma=False,
    )
```

```python
import functools
import math

import jax
import jax.numpy as jnp
from jax import lax
from jax.experimental import pallas as pl
from jax.experimental.pallas import tpu as pltpu
from jax.sharding import PartitionSpec as P

BLOCK = 128
SUBS = 2
MESH = pl.DeviceIdType.MESH
GELU_C = math.sqrt(2.0 / math.pi)
GELU_A = 0.044715
F32 = jnp.float32
BF16 = jnp.bfloat16


def gelu(v):
    return v * (0.5 * (1.0 + jnp.tanh(GELU_C * (v + GELU_A * (v * v * v)))))


def gelu_and_slope(v):
    squared = v * v
    t = jnp.tanh(GELU_C * (v + GELU_A * (squared * v)))
    share = 0.5 * (1.0 + t)
    slope = share + v * (0.5 * (1.0 - t * t) * (GELU_C * (1.0 + 3.0 * GELU_A * squared)))
    return v * share, slope


def dot(a, b):
    return jnp.dot(a, b, preferred_element_type=F32)


def kernel(
    n, sections, stream_ref, grad_ref, now_ref, back_ref, w_ref, mask_ref,
    out_v, pg_v, wg_v,
    mask_s, w_v, now_v, back_v, own_grad, own_stream, part32, part16, hop_in, hop_out, pieces, gathered,
    fan_out, fan_in, total_v, slope_v, hidden_t, gh_v,
    load_sem, hop_recv, ring_send, ring_recv, piece_send, piece_recv, fan_recv, relay_sem, late_sem,
):
    hidden, width = w_v.shape
    half = width // 2
    sub = half // SUBS
    tokens = gathered.shape[1]
    mine = own_grad.shape[0]
    rows = n * mine
    reach = n // 2
    blk = lax.axis_index("blk")
    section = lax.axis_index("section")
    place = (lax.rem(blk, n), lax.div(blk, n))

    def wrap(v):
        return lax.rem(v + 2 * n, n)

    def device(axis, at, where):
        index = place[1] * n + at if axis == 0 else at * n + place[0]
        return {"blk": index, "section": where}

    def half_columns(h):
        return pl.ds(h * half, half)

    def sub_columns(c):
        return pl.ds(c * sub, sub)

    def block_rows(b):
        return pl.ds(pl.multiple_of(b * rows, rows), rows)

    loads = [
        pltpu.make_async_copy(now_ref.at[0], now_v, load_sem.at[0]),
        pltpu.make_async_copy(mask_ref.at[0], mask_s, load_sem.at[1]),
        pltpu.make_async_copy(grad_ref.at[0], own_grad, load_sem.at[2]),
        pltpu.make_async_copy(back_ref.at[0], back_v, load_sem.at[3]),
    ]
    w_loads = []
    for chunk in range(2 * SUBS):
        columns = pl.ds(chunk * sub, sub)
        w_loads.append(pltpu.make_async_copy(w_ref.at[0, :, columns], w_v.at[:, columns], load_sem.at[4 + chunk]))
    for copy in loads[:2] + w_loads + loads[2:]:
        copy.start()

    barrier = pltpu.get_barrier_semaphore()
    order = sorted(range(1, n), key=lambda offset: -min(offset, n - offset))
    first, last = section == 0, section == sections - 1
    in_line = jnp.logical_or(place[0] == 0, place[1] == 0)
    is_late = jnp.logical_and(first, blk == 0)
    meets_late = jnp.logical_and(in_line, jnp.logical_and(section <= 1, jnp.logical_not(is_late)))
    feeds_late = jnp.logical_and(in_line, section == 1)

    def to_late(h, way):
        onto = wrap(place[h] + 1 - 2 * way) == 0
        return jnp.logical_and(first, jnp.logical_and(place[1 - h] == 0, onto))

    beside_late = functools.reduce(jnp.logical_or, [to_late(h, way) for h in range(2) for way in range(2)])

    def announce_to_senders(sem):
        for offset in order:
            for axis in range(2):
                at = wrap(place[axis] + offset)
                pl.semaphore_signal(sem, inc=1, device_id=device(axis, at, section), device_id_type=MESH)

        @pl.when(section < sections - 1)
        def _():
            pl.semaphore_signal(sem, inc=1, device_id=device(0, place[0], section + 1), device_id_type=MESH)
            for offset in order:
                for axis in range(2):
                    at = wrap(place[axis] + offset)
                    pl.semaphore_signal(sem, inc=1, device_id=device(axis, at, section + 1), device_id_type=MESH)

    expected = 2 * (n - 1) + jnp.where(first, 0, 2 * n - 1) + jnp.where(last, 0, 1) - jnp.where(meets_late, 1, 0)
    expected = expected + jnp.where(is_late, 2 * (n - 1), 0)

    @pl.when(jnp.logical_not(is_late))
    def _():
        announce_to_senders(barrier)

    @pl.when(section > 0)
    def _():
        pl.semaphore_signal(barrier, inc=1, device_id=device(0, place[0], section - 1), device_id_type=MESH)

    @pl.when(jnp.logical_and(feeds_late, blk > 0))
    def _():
        pl.semaphore_signal(barrier, inc=1, device_id={"blk": 0, "section": section - 1}, device_id_type=MESH)

    @pl.when(is_late)
    def _():
        pl.semaphore_wait(barrier, expected)
        announce_to_senders(late_sem)

    def mask_tile(i, j):
        return jnp.full((BLOCK, BLOCK), mask_s[i, j].astype(F32), F32)

    to_row = lax.broadcasted_iota(jnp.int32, (tokens, tokens), 0)
    from_row = lax.broadcasted_iota(jnp.int32, (tokens, tokens), 1)
    shift_rows, shift_mine = rows.bit_length() - 1, mine.bit_length() - 1
    wanted = (
        ((to_row & (rows - 1)) >> shift_mine) * rows + (to_row >> shift_rows) * mine + (to_row & (mine - 1))
    )
    permute = jnp.where(from_row == wanted, 1.0, 0.0).astype(BF16)

    loads[0].wait()
    hidden_now = gelu(now_v[...].astype(F32)).astype(BF16)
    hidden_half = (dot(permute, hidden_now).astype(BF16), hidden_now)
    def forward(c):
        for h in range(2):
            chunk = h * SUBS + c
            w_loads[chunk].wait()
            for j in range(chunk * sub // BLOCK, (chunk + 1) * sub // BLOCK):
                for i in range(hidden // BLOCK):
                    tile = (pl.ds(i * BLOCK, BLOCK), pl.ds(j * BLOCK, BLOCK))
                    w_v[tile] = w_v[tile] * mask_tile(i, j).astype(BF16)
            product = dot(hidden_half[h], w_v[:, chunk * sub : (chunk + 1) * sub])
            part32[h, :, c * sub : (c + 1) * sub] = product
            part16[h, :, c * sub : (c + 1) * sub] = product.astype(BF16)

    loads[1].wait()
    forward(0)
    loads[2].wait()

    @pl.when(jnp.logical_not(is_late))
    def _():
        pl.semaphore_wait(barrier, expected)

    def piece_copy(h, at, where, slot):
        return pltpu.make_async_remote_copy(
            src_ref=own_grad.at[:, half_columns(h)],
            dst_ref=pieces.at[h, place[h]],
            send_sem=piece_send.at[slot],
            recv_sem=piece_recv.at[h],
            device_id=device(h, at, where),
            device_id_type=MESH,
        )

    before = jnp.maximum(section - 1, 0)
    after = jnp.minimum(section + 1, sections - 1)

    @pl.when(section > 0)
    def _():
        for offset in order + [0]:
            for h in range(2):
                at = wrap(place[h] + offset)
                held_back = jnp.logical_and(section == 1, jnp.logical_and(place[1 - h] == 0, at == 0))

                @pl.when(jnp.logical_not(held_back))
                def _():
                    piece_copy(h, at, before, 0).start()

    own_pieces = [
        pltpu.make_async_copy(own_grad.at[:, half_columns(h)], pieces.at[h, place[h]], relay_sem.at[2 + h])
        for h in range(2)
    ]

    @pl.when(last)
    def _():
        for offset in order:
            for h in range(2):
                piece_copy(h, wrap(place[h] + offset), section, 1).start()
        for copy in own_pieces:
            copy.start()

    steps_of = lambda c, way: reach if way == 1 else reach - 1
    chains = [(h, c, way) for c in range(SUBS) for h in range(2) for way in range(2)]

    def hop_copy(h, c, way, step):
        turn = 1 - 2 * way
        target = wrap(place[h] + turn * (steps_of(c, way) - step + 1))
        if step == 1:
            source = part16.at[h, block_rows(target), sub_columns(c)]
        else:
            source = hop_out.at[h, way, step - 2, :, sub_columns(c)]
        return pltpu.make_async_remote_copy(
            src_ref=source,
            dst_ref=hop_in.at[h, way, step - 1, :, sub_columns(c)],
            send_sem=ring_send.at[0],
            recv_sem=hop_recv.at[h, c, way, step - 1],
            device_id=device(h, wrap(place[h] + turn), section),
            device_id_type=MESH,
        )

    for c in range(SUBS):
        if c > 0:
            forward(c)
        for h in range(2):
            for way in range(2):
                if steps_of(c, way) >= 1:

                    @pl.when(jnp.logical_not(to_late(h, way)))
                    def _():
                        hop_copy(h, c, way, 1).start()

    relay_copy = pltpu.make_async_remote_copy(
        src_ref=stream_ref.at[0],
        dst_ref=own_stream,
        send_sem=relay_sem.at[0],
        recv_sem=relay_sem.at[1],
        device_id=device(0, place[0], after),
        device_id_type=MESH,
    )
    stream_copy = pltpu.make_async_copy(stream_ref.at[0], own_stream, relay_sem.at[4])

    @pl.when(section < sections - 1)
    def _():
        relay_copy.start()

    @pl.when(first)
    def _():
        stream_copy.start()

    loads[3].wait()
    hidden_back, slope = gelu_and_slope(back_v[...].astype(F32))
    slope_v[...] = slope
    transposed = jnp.transpose(hidden_back).astype(BF16)
    hidden_t[0] = transposed
    hidden_t[1] = dot(transposed, permute).astype(BF16)

    def ring_copy(h, c, way, step):
        turn = 1 - 2 * way
        region = gathered.at[h, block_rows(wrap(place[1 - h] - turn * (step - 1))), sub_columns(c)]
        return pltpu.make_async_remote_copy(
            src_ref=region,
            dst_ref=region,
            send_sem=ring_send.at[1],
            recv_sem=ring_recv.at[h, c, way, step - 1],
            device_id=device(1 - h, wrap(place[1 - h] + turn), section),
            device_id_type=MESH,
        )

    def ring_arrival(h, c, way, step):
        turn = 1 - 2 * way
        region = gathered.at[h, block_rows(wrap(place[1 - h] - turn * step)), sub_columns(c)]
        return pltpu.make_async_remote_copy(
            src_ref=region,
            dst_ref=region,
            send_sem=ring_send.at[1],
            recv_sem=ring_recv.at[h, c, way, step - 1],
            device_id=device(1 - h, wrap(place[1 - h] + turn), section),
            device_id_type=MESH,
        )

    def waiter(region, sem):
        return pltpu.make_async_remote_copy(
            src_ref=region,
            dst_ref=region,
            send_sem=sem,
            recv_sem=sem,
            device_id=device(0, place[0], after),
            device_id_type=MESH,
        )

    def hop_onward(h, c, way, step):
        turn = 1 - 2 * way
        hop_copy(h, c, way, step - 1).wait_recv()
        target = wrap(place[h] + turn * (steps_of(c, way) - step + 1))
        cols = slice(c * sub, (c + 1) * sub)
        total = hop_in[h, way, step - 2, :, cols].astype(F32) + part32[h, block_rows(target), cols]
        hop_out[h, way, step - 2, :, cols] = total.astype(BF16)
        hop_copy(h, c, way, step).start()

    def ring_onward(h, c, way, step):
        ring_arrival(h, c, way, step - 1).wait_recv()
        ring_copy(h, c, way, step).start()

    def start_ring():
        @pl.when(last)
        def _():
            for h in range(2):
                own_pieces[h].wait()
                waiter(pieces.at[h, pl.ds(0, n - 1)], piece_recv.at[h]).wait_recv()

        @pl.when(section < sections - 1)
        def _():
            for h in range(2):
                waiter(pieces.at[h], piece_recv.at[h]).wait_recv()

        for h in range(2):
            block = jnp.concatenate([pieces[h, at].astype(F32) for at in range(n)], axis=0)
            gathered[h, block_rows(place[1 - h]), :] = block.astype(BF16)
        for h, c, way in chains:
            if steps_of(c, way) >= 1:
                ring_copy(h, c, way, 1).start()

    @pl.when(beside_late)
    def _():
        pl.semaphore_wait(late_sem, 1)
        for h, c, way in chains:
            if steps_of(c, way) >= 1:

                @pl.when(to_late(h, way))
                def _():
                    hop_copy(h, c, way, 1).start()

    for step in range(2, reach + 1):
        for c in range(SUBS):
            for chain in chains:
                if chain[1] == c and steps_of(*chain[1:]) >= step:
                    hop_onward(*chain, step)
            if step > 2:
                for chain in chains:
                    if chain[1] == c and steps_of(*chain[1:]) >= step - 1:
                        ring_onward(*chain, step - 1)
        if step == 2:
            start_ring()

            @pl.when(feeds_late)
            def _():
                pl.semaphore_wait(late_sem, 1)
                for h in range(2):

                    @pl.when(place[1 - h] == 0)
                    def _():
                        piece_copy(h, 0, before, 0).start()

    def fan_copy(h, offset):
        at = wrap(place[1 - h] + offset)
        return pltpu.make_async_remote_copy(
            src_ref=fan_out.at[h, at],
            dst_ref=fan_in.at[h, place[1 - h]],
            send_sem=ring_send.at[2],
            recv_sem=fan_recv.at[h],
            device_id=device(1 - h, at, section),
            device_id_type=MESH,
        )

    @pl.when(jnp.logical_and(meets_late, jnp.logical_not(jnp.logical_or(feeds_late, beside_late))))
    def _():
        pl.semaphore_wait(late_sem, 1)

    for h in range(2):
        for c in range(SUBS):
            cols = slice(c * sub, (c + 1) * sub)
            total = part32[h, block_rows(place[h]), cols]
            for way in range(2):
                if steps_of(c, way) >= 1:
                    hop_copy(h, c, way, steps_of(c, way)).wait_recv()
                    total = total + hop_in[h, way, steps_of(c, way) - 1, :, cols].astype(F32)
            for at in range(n):
                total_v[h, at, :, cols] = total[at * mine : (at + 1) * mine, :]
                fan_out[h, at, :, cols] = total[at * mine : (at + 1) * mine, :].astype(BF16)
        for offset in order:
            fan_copy(h, offset).start()

    for chain in chains:
        if steps_of(*chain[1:]) >= reach:
            ring_onward(*chain, reach)

    contract_last = (((1,), (1,)), ((), ()))
    for c in range(SUBS):
        for h in range(2):
            for way in range(2):
                if steps_of(c, way) >= 1:
                    ring_arrival(h, c, way, steps_of(c, way)).wait_recv()
            arrived = gathered[h, :, c * sub : (c + 1) * sub]
            start = h * half + c * sub
            product = lax.dot_general(
                arrived, w_v[:, start : start + sub], contract_last, preferred_element_type=F32
            )
            gh_v[h] = product if c == 0 else gh_v[h] + product
            product = dot(hidden_t[h], arrived)
            for j in range(sub // BLOCK):
                for i in range(hidden // BLOCK):
                    column = start // BLOCK + j
                    tile = product[i * BLOCK : (i + 1) * BLOCK, j * BLOCK : (j + 1) * BLOCK] * mask_tile(i, column)
                    wg_v[pl.ds(i * BLOCK, BLOCK), pl.ds(column * BLOCK, BLOCK)] = tile.astype(BF16)
    pack = 16 // mine
    for group in range(tokens // 16):
        found = []
        for part in range(pack):
            along_y, along_x = divmod(group * pack + part, n)
            found.append(gh_v[1, pl.ds(along_x * rows + along_y * mine, mine), :])
        here = pl.ds(group * 16, 16)
        pg_v[here, :] = ((gh_v[0, here, :] + jnp.concatenate(found, axis=0)) * slope_v[here, :]).astype(BF16)

    @pl.when(section < sections - 1)
    def _():
        relay_copy.wait_send()

    @pl.when(section > 0)
    def _():
        relay_copy.wait_recv()

    @pl.when(first)
    def _():
        stream_copy.wait()

    for h in range(2):
        waiter(fan_in.at[h, pl.ds(0, n - 1)], fan_recv.at[h]).wait_recv()
        total = own_stream[:, h * half : (h + 1) * half].astype(F32) + total_v[h, place[1 - h]]
        for offset in range(1, n):
            total = total + fan_in[h, wrap(place[1 - h] + offset)].astype(F32)
        out_v[:, h * half : (h + 1) * half] = total.astype(BF16)

    @pl.when(section > 0)
    def _():
        for h in range(2):
            waiter(pieces.at[h], piece_send.at[0]).wait_send()

    @pl.when(last)
    def _():
        for h in range(2):
            waiter(pieces.at[h, pl.ds(0, n - 1)], piece_send.at[1]).wait_send()

    for h in range(2):
        waiter(gathered.at[h, pl.ds(0, (n - 1) * rows)], ring_send.at[0]).wait_send()
        waiter(gathered.at[h, pl.ds(0, (n - 1) * rows)], ring_send.at[1]).wait_send()
        waiter(fan_in.at[h, pl.ds(0, n - 1)], ring_send.at[2]).wait_send()


def store_kernel(*refs):
    copies = [pltpu.make_async_copy(refs[k], refs[3 + k].at[0], refs[6].at[k]) for k in range(3)]
    for copy in copies:
        copy.start()
    for copy in copies:
        copy.wait()


def body(n, sections, stream_sent, grad_sent, preact_now, preact_back, down_weight, block_mask):
    mine, width = stream_sent.shape[1:]
    tokens, hidden = preact_now.shape[1:]
    half = width // 2
    rows, reach = n * mine, n // 2
    anywhere = pl.BlockSpec(memory_space=pl.ANY)
    dma = pltpu.SemaphoreType.DMA
    held = pl.pallas_call(
        functools.partial(kernel, n, sections),
        name="relay_layer",
        out_shape=(
            pltpu.VMEM((mine, width), BF16),
            pltpu.VMEM((tokens, hidden), BF16),
            pltpu.VMEM((hidden, width), BF16),
        ),
        in_specs=[anywhere] * 6,
        out_specs=(pl.BlockSpec(memory_space=pltpu.VMEM),) * 3,
        scratch_shapes=[
            pltpu.SMEM(block_mask.shape[1:], jnp.int32),
            pltpu.VMEM((hidden, width), BF16),
            pltpu.VMEM((tokens, hidden), BF16),
            pltpu.VMEM((tokens, hidden), BF16),
            pltpu.VMEM((mine, width), BF16),
            pltpu.VMEM((mine, width), BF16),
            pltpu.VMEM((2, tokens, half), F32),
            pltpu.VMEM((2, tokens, half), BF16),
            pltpu.VMEM((2, 2, reach, rows, half), BF16),
            pltpu.VMEM((2, 2, reach - 1, rows, half), BF16),
            pltpu.VMEM((2, n, mine, half), BF16),
            pltpu.VMEM((2, tokens, half), BF16),
            pltpu.VMEM((2, n, mine, half), BF16),
            pltpu.VMEM((2, n, mine, half), BF16),
            pltpu.VMEM((2, n, mine, half), F32),
            pltpu.VMEM((tokens, hidden), F32),
            pltpu.VMEM((2, hidden, tokens), BF16),
            pltpu.VMEM((2, tokens, hidden), F32),
            dma((4 + 2 * SUBS,)),
            dma((2, SUBS, 2, reach)),
            dma((3,)),
            dma((2, SUBS, 2, reach)),
            dma((2,)),
            dma((2,)),
            dma((2,)),
            dma((5,)),
            pltpu.SemaphoreType.REGULAR,
        ],
        compiler_params=pltpu.CompilerParams(collective_id=0, has_side_effects=True),
    )(stream_sent, grad_sent, preact_now, preact_back, down_weight, block_mask)
    return pl.pallas_call(
        store_kernel,
        name="store_outputs",
        out_shape=(
            jax.ShapeDtypeStruct(stream_sent.shape, BF16),
            jax.ShapeDtypeStruct(preact_back.shape, BF16),
            jax.ShapeDtypeStruct(down_weight.shape, BF16),
        ),
        in_specs=[pl.BlockSpec(memory_space=pltpu.VMEM)] * 3,
        out_specs=(anywhere,) * 3,
        scratch_shapes=[dma((3,))],
    )(*[pltpu.with_memory_space_constraint(a, pltpu.VMEM) for a in held])


def solution(mesh):
    n = math.isqrt(mesh.shape["blk"])
    placed = (
        P("section", "blk", None),
        P("section", "blk", None),
        P("section", None, "blk"),
        P("section", None, "blk"),
        P("section", "blk", None),
        P("section", "blk", None),
    )
    return jax.shard_map(
        functools.partial(body, n, mesh.shape["section"]),
        mesh=mesh,
        in_specs=placed,
        out_specs=(P("section", "blk", None), P("section", None, "blk"), P("section", "blk", None)),
        check_vma=False,
    )
```

```python
import functools
import math

import jax
import jax.numpy as jnp
from jax import lax
from jax.experimental import pallas as pl
from jax.experimental.pallas import tpu as pltpu
from jax.sharding import PartitionSpec as P

BLOCK = 128
SUBS = 2
MESH = pl.DeviceIdType.MESH
GELU_C = math.sqrt(2.0 / math.pi)
GELU_A = 0.044715
F32 = jnp.float32
BF16 = jnp.bfloat16


def gelu(v):
    return v * (0.5 * (1.0 + jnp.tanh(GELU_C * (v + GELU_A * (v * v * v)))))


def gelu_and_slope(v):
    squared = v * v
    t = jnp.tanh(GELU_C * (v + GELU_A * (squared * v)))
    share = 0.5 * (1.0 + t)
    slope = share + v * (0.5 * (1.0 - t * t) * (GELU_C * (1.0 + 3.0 * GELU_A * squared)))
    return v * share, slope


def dot(a, b):
    return jnp.dot(a, b, preferred_element_type=F32)


def kernel(
    n, sections, stream_ref, grad_ref, now_ref, back_ref, w_ref, mask_ref,
    out_v, pg_v, wg_v,
    mask_s, w_v, now_v, back_v, own_grad, own_stream, part32, part16, hop_in, hop_out, pieces, gathered,
    fan_out, fan_in, total_v, slope_v, hidden_t, gh_v,
    load_sem, hop_recv, ring_send, ring_recv, piece_send, piece_recv, fan_recv, relay_sem, late_sem,
):
    hidden, width = w_v.shape
    half = width // 2
    sub = half // SUBS
    tokens = gathered.shape[1]
    mine = own_grad.shape[0]
    rows = n * mine
    reach = n // 2
    blk = lax.axis_index("blk")
    section = lax.axis_index("section")
    place = (lax.rem(blk, n), lax.div(blk, n))

    def wrap(v):
        return lax.rem(v + 2 * n, n)

    def device(axis, at, where):
        index = place[1] * n + at if axis == 0 else at * n + place[0]
        return {"blk": index, "section": where}

    def half_columns(h):
        return pl.ds(h * half, half)

    def sub_columns(c):
        return pl.ds(c * sub, sub)

    def block_rows(b):
        return pl.ds(pl.multiple_of(b * rows, rows), rows)

    loads = [
        pltpu.make_async_copy(now_ref.at[0], now_v, load_sem.at[0]),
        pltpu.make_async_copy(mask_ref.at[0], mask_s, load_sem.at[1]),
        pltpu.make_async_copy(grad_ref.at[0], own_grad, load_sem.at[2]),
        pltpu.make_async_copy(back_ref.at[0], back_v, load_sem.at[3]),
    ]
    w_loads = []
    for chunk in range(2 * SUBS):
        columns = pl.ds(chunk * sub, sub)
        w_loads.append(pltpu.make_async_copy(w_ref.at[0, :, columns], w_v.at[:, columns], load_sem.at[4 + chunk]))
    for copy in loads[:2] + w_loads + loads[2:]:
        copy.start()

    barrier = pltpu.get_barrier_semaphore()
    order = sorted(range(1, n), key=lambda offset: -min(offset, n - offset))
    first, last = section == 0, section == sections - 1
    in_line = jnp.logical_or(place[0] == 0, place[1] == 0)
    is_late = jnp.logical_and(first, blk == 0)
    meets_late = jnp.logical_and(in_line, jnp.logical_and(section <= 1, jnp.logical_not(is_late)))
    feeds_late = jnp.logical_and(in_line, section == 1)

    def to_late(h, way):
        onto = wrap(place[h] + 1 - 2 * way) == 0
        return jnp.logical_and(first, jnp.logical_and(place[1 - h] == 0, onto))

    beside_late = functools.reduce(jnp.logical_or, [to_late(h, way) for h in range(2) for way in range(2)])

    def announce_to_senders(sem):
        for offset in order:
            for axis in range(2):
                at = wrap(place[axis] + offset)
                pl.semaphore_signal(sem, inc=1, device_id=device(axis, at, section), device_id_type=MESH)

        @pl.when(section < sections - 1)
        def _():
            pl.semaphore_signal(sem, inc=1, device_id=device(0, place[0], section + 1), device_id_type=MESH)
            for offset in order:
                for axis in range(2):
                    at = wrap(place[axis] + offset)
                    pl.semaphore_signal(sem, inc=1, device_id=device(axis, at, section + 1), device_id_type=MESH)

    expected = 2 * (n - 1) + jnp.where(first, 0, 2 * n - 1) + jnp.where(last, 0, 1) - jnp.where(meets_late, 1, 0)
    expected = expected + jnp.where(is_late, 2 * (n - 1), 0)

    @pl.when(jnp.logical_not(is_late))
    def _():
        announce_to_senders(barrier)

    @pl.when(section > 0)
    def _():
        pl.semaphore_signal(barrier, inc=1, device_id=device(0, place[0], section - 1), device_id_type=MESH)

    @pl.when(jnp.logical_and(feeds_late, blk > 0))
    def _():
        pl.semaphore_signal(barrier, inc=1, device_id={"blk": 0, "section": section - 1}, device_id_type=MESH)

    @pl.when(is_late)
    def _():
        pl.semaphore_wait(barrier, expected)
        announce_to_senders(late_sem)

    def mask_tile(i, j):
        return jnp.full((BLOCK, BLOCK), mask_s[i, j].astype(F32), F32)

    to_row = lax.broadcasted_iota(jnp.int32, (tokens, tokens), 0)
    from_row = lax.broadcasted_iota(jnp.int32, (tokens, tokens), 1)
    shift_rows, shift_mine = rows.bit_length() - 1, mine.bit_length() - 1
    wanted = (
        ((to_row & (rows - 1)) >> shift_mine) * rows + (to_row >> shift_rows) * mine + (to_row & (mine - 1))
    )
    permute = jnp.where(from_row == wanted, 1.0, 0.0).astype(BF16)

    loads[0].wait()
    hidden_now = gelu(now_v[...].astype(F32)).astype(BF16)
    hidden_half = (dot(permute, hidden_now).astype(BF16), hidden_now)
    def forward(c):
        for h in range(2):
            chunk = h * SUBS + c
            w_loads[chunk].wait()
            for j in range(chunk * sub // BLOCK, (chunk + 1) * sub // BLOCK):
                for i in range(hidden // BLOCK):
                    tile = (pl.ds(i * BLOCK, BLOCK), pl.ds(j * BLOCK, BLOCK))
                    w_v[tile] = w_v[tile] * mask_tile(i, j).astype(BF16)
            product = dot(hidden_half[h], w_v[:, chunk * sub : (chunk + 1) * sub])
            part32[h, :, c * sub : (c + 1) * sub] = product
            part16[h, :, c * sub : (c + 1) * sub] = product.astype(BF16)

    loads[1].wait()
    forward(0)
    loads[2].wait()

    @pl.when(jnp.logical_not(is_late))
    def _():
        pl.semaphore_wait(barrier, expected)

    def piece_copy(h, at, where, slot):
        return pltpu.make_async_remote_copy(
            src_ref=own_grad.at[:, half_columns(h)],
            dst_ref=pieces.at[h, place[h]],
            send_sem=piece_send.at[slot],
            recv_sem=piece_recv.at[h],
            device_id=device(h, at, where),
            device_id_type=MESH,
        )

    before = jnp.maximum(section - 1, 0)
    after = jnp.minimum(section + 1, sections - 1)

    @pl.when(section > 0)
    def _():
        for offset in order + [0]:
            for h in range(2):
                at = wrap(place[h] + offset)
                held_back = jnp.logical_and(section == 1, jnp.logical_and(place[1 - h] == 0, at == 0))

                @pl.when(jnp.logical_not(held_back))
                def _():
                    piece_copy(h, at, before, 0).start()

    own_pieces = [
        pltpu.make_async_copy(own_grad.at[:, half_columns(h)], pieces.at[h, place[h]], relay_sem.at[2 + h])
        for h in range(2)
    ]

    @pl.when(last)
    def _():
        for offset in order:
            for h in range(2):
                piece_copy(h, wrap(place[h] + offset), section, 1).start()
        for copy in own_pieces:
            copy.start()

    steps_of = lambda c, way: reach if (c + way) % 2 == 0 else reach - 1
    ring_steps_of = lambda c, way: reach if way == 1 else reach - 1
    chains = [(h, c, way) for c in range(SUBS) for h in range(2) for way in range(2)]

    def hop_copy(h, c, way, step):
        turn = 1 - 2 * way
        target = wrap(place[h] + turn * (steps_of(c, way) - step + 1))
        if step == 1:
            source = part16.at[h, block_rows(target), sub_columns(c)]
        else:
            source = hop_out.at[h, way, step - 2, :, sub_columns(c)]
        return pltpu.make_async_remote_copy(
            src_ref=source,
            dst_ref=hop_in.at[h, way, step - 1, :, sub_columns(c)],
            send_sem=ring_send.at[0],
            recv_sem=hop_recv.at[h, c, way, step - 1],
            device_id=device(h, wrap(place[h] + turn), section),
            device_id_type=MESH,
        )

    for c in range(SUBS):
        if c > 0:
            forward(c)
        for h in range(2):
            for way in range(2):
                if steps_of(c, way) >= 1:

                    @pl.when(jnp.logical_not(to_late(h, way)))
                    def _():
                        hop_copy(h, c, way, 1).start()

    relay_copy = pltpu.make_async_remote_copy(
        src_ref=stream_ref.at[0],
        dst_ref=own_stream,
        send_sem=relay_sem.at[0],
        recv_sem=relay_sem.at[1],
        device_id=device(0, place[0], after),
        device_id_type=MESH,
    )
    stream_copy = pltpu.make_async_copy(stream_ref.at[0], own_stream, relay_sem.at[4])

    @pl.when(section < sections - 1)
    def _():
        relay_copy.start()

    @pl.when(first)
    def _():
        stream_copy.start()

    loads[3].wait()
    hidden_back, slope = gelu_and_slope(back_v[...].astype(F32))
    slope_v[...] = slope
    transposed = jnp.transpose(hidden_back).astype(BF16)
    hidden_t[0] = transposed
    hidden_t[1] = dot(transposed, permute).astype(BF16)

    def ring_copy(h, c, way, step):
        turn = 1 - 2 * way
        region = gathered.at[h, block_rows(wrap(place[1 - h] - turn * (step - 1))), sub_columns(c)]
        return pltpu.make_async_remote_copy(
            src_ref=region,
            dst_ref=region,
            send_sem=ring_send.at[1],
            recv_sem=ring_recv.at[h, c, way, step - 1],
            device_id=device(1 - h, wrap(place[1 - h] + turn), section),
            device_id_type=MESH,
        )

    def ring_arrival(h, c, way, step):
        turn = 1 - 2 * way
        region = gathered.at[h, block_rows(wrap(place[1 - h] - turn * step)), sub_columns(c)]
        return pltpu.make_async_remote_copy(
            src_ref=region,
            dst_ref=region,
            send_sem=ring_send.at[1],
            recv_sem=ring_recv.at[h, c, way, step - 1],
            device_id=device(1 - h, wrap(place[1 - h] + turn), section),
            device_id_type=MESH,
        )

    def waiter(region, sem):
        return pltpu.make_async_remote_copy(
            src_ref=region,
            dst_ref=region,
            send_sem=sem,
            recv_sem=sem,
            device_id=device(0, place[0], after),
            device_id_type=MESH,
        )

    def hop_onward(h, c, way, step):
        turn = 1 - 2 * way
        hop_copy(h, c, way, step - 1).wait_recv()
        target = wrap(place[h] + turn * (steps_of(c, way) - step + 1))
        cols = slice(c * sub, (c + 1) * sub)
        total = hop_in[h, way, step - 2, :, cols].astype(F32) + part32[h, block_rows(target), cols]
        hop_out[h, way, step - 2, :, cols] = total.astype(BF16)
        hop_copy(h, c, way, step).start()

    def ring_onward(h, c, way, step):
        ring_arrival(h, c, way, step - 1).wait_recv()
        ring_copy(h, c, way, step).start()

    def start_ring():
        @pl.when(last)
        def _():
            for h in range(2):
                own_pieces[h].wait()
                waiter(pieces.at[h, pl.ds(0, n - 1)], piece_recv.at[h]).wait_recv()

        @pl.when(section < sections - 1)
        def _():
            for h in range(2):
                waiter(pieces.at[h], piece_recv.at[h]).wait_recv()

        for h in range(2):
            block = jnp.concatenate([pieces[h, at].astype(F32) for at in range(n)], axis=0)
            gathered[h, block_rows(place[1 - h]), :] = block.astype(BF16)
        for h, c, way in chains:
            if ring_steps_of(c, way) >= 1:
                ring_copy(h, c, way, 1).start()

    @pl.when(beside_late)
    def _():
        pl.semaphore_wait(late_sem, 1)
        for h, c, way in chains:
            if steps_of(c, way) >= 1:

                @pl.when(to_late(h, way))
                def _():
                    hop_copy(h, c, way, 1).start()

    for step in range(2, reach + 1):
        for c in range(SUBS):
            for chain in chains:
                if chain[1] == c and steps_of(*chain[1:]) >= step:
                    hop_onward(*chain, step)
            if step > 2:
                for chain in chains:
                    if chain[1] == c and ring_steps_of(*chain[1:]) >= step - 1:
                        ring_onward(*chain, step - 1)
        if step == 2:
            start_ring()

            @pl.when(feeds_late)
            def _():
                pl.semaphore_wait(late_sem, 1)
                for h in range(2):

                    @pl.when(place[1 - h] == 0)
                    def _():
                        piece_copy(h, 0, before, 0).start()

    def fan_copy(h, offset):
        at = wrap(place[1 - h] + offset)
        return pltpu.make_async_remote_copy(
            src_ref=fan_out.at[h, at],
            dst_ref=fan_in.at[h, place[1 - h]],
            send_sem=ring_send.at[2],
            recv_sem=fan_recv.at[h],
            device_id=device(1 - h, at, section),
            device_id_type=MESH,
        )

    @pl.when(jnp.logical_and(meets_late, jnp.logical_not(jnp.logical_or(feeds_late, beside_late))))
    def _():
        pl.semaphore_wait(late_sem, 1)

    for h in range(2):
        for c in range(SUBS):
            cols = slice(c * sub, (c + 1) * sub)
            total = part32[h, block_rows(place[h]), cols]
            for way in range(2):
                if steps_of(c, way) >= 1:
                    hop_copy(h, c, way, steps_of(c, way)).wait_recv()
                    total = total + hop_in[h, way, steps_of(c, way) - 1, :, cols].astype(F32)
            for at in range(n):
                total_v[h, at, :, cols] = total[at * mine : (at + 1) * mine, :]
                fan_out[h, at, :, cols] = total[at * mine : (at + 1) * mine, :].astype(BF16)
        for offset in order:
            fan_copy(h, offset).start()

    for chain in chains:
        if ring_steps_of(*chain[1:]) >= reach:
            ring_onward(*chain, reach)

    contract_last = (((1,), (1,)), ((), ()))
    for c in range(SUBS):
        for h in range(2):
            for way in range(2):
                if ring_steps_of(c, way) >= 1:
                    ring_arrival(h, c, way, ring_steps_of(c, way)).wait_recv()
            arrived = gathered[h, :, c * sub : (c + 1) * sub]
            start = h * half + c * sub
            product = lax.dot_general(
                arrived, w_v[:, start : start + sub], contract_last, preferred_element_type=F32
            )
            gh_v[h] = product if c == 0 else gh_v[h] + product
            product = dot(hidden_t[h], arrived)
            for j in range(sub // BLOCK):
                for i in range(hidden // BLOCK):
                    column = start // BLOCK + j
                    tile = product[i * BLOCK : (i + 1) * BLOCK, j * BLOCK : (j + 1) * BLOCK] * mask_tile(i, column)
                    wg_v[pl.ds(i * BLOCK, BLOCK), pl.ds(column * BLOCK, BLOCK)] = tile.astype(BF16)
    pack = 16 // mine
    for group in range(tokens // 16):
        found = []
        for part in range(pack):
            along_y, along_x = divmod(group * pack + part, n)
            found.append(gh_v[1, pl.ds(along_x * rows + along_y * mine, mine), :])
        here = pl.ds(group * 16, 16)
        pg_v[here, :] = ((gh_v[0, here, :] + jnp.concatenate(found, axis=0)) * slope_v[here, :]).astype(BF16)

    @pl.when(section < sections - 1)
    def _():
        relay_copy.wait_send()

    @pl.when(section > 0)
    def _():
        relay_copy.wait_recv()

    @pl.when(first)
    def _():
        stream_copy.wait()

    for h in range(2):
        waiter(fan_in.at[h, pl.ds(0, n - 1)], fan_recv.at[h]).wait_recv()
        total = own_stream[:, h * half : (h + 1) * half].astype(F32) + total_v[h, place[1 - h]]
        for offset in range(1, n):
            total = total + fan_in[h, wrap(place[1 - h] + offset)].astype(F32)
        out_v[:, h * half : (h + 1) * half] = total.astype(BF16)

    @pl.when(section > 0)
    def _():
        for h in range(2):
            waiter(pieces.at[h], piece_send.at[0]).wait_send()

    @pl.when(last)
    def _():
        for h in range(2):
            waiter(pieces.at[h, pl.ds(0, n - 1)], piece_send.at[1]).wait_send()

    for h in range(2):
        waiter(gathered.at[h, pl.ds(0, (n - 1) * rows)], ring_send.at[0]).wait_send()
        waiter(gathered.at[h, pl.ds(0, (n - 1) * rows)], ring_send.at[1]).wait_send()
        waiter(fan_in.at[h, pl.ds(0, n - 1)], ring_send.at[2]).wait_send()


def store_kernel(*refs):
    copies = [pltpu.make_async_copy(refs[k], refs[3 + k].at[0], refs[6].at[k]) for k in range(3)]
    for copy in copies:
        copy.start()
    for copy in copies:
        copy.wait()


def body(n, sections, stream_sent, grad_sent, preact_now, preact_back, down_weight, block_mask):
    mine, width = stream_sent.shape[1:]
    tokens, hidden = preact_now.shape[1:]
    half = width // 2
    rows, reach = n * mine, n // 2
    anywhere = pl.BlockSpec(memory_space=pl.ANY)
    dma = pltpu.SemaphoreType.DMA
    held = pl.pallas_call(
        functools.partial(kernel, n, sections),
        name="relay_layer",
        out_shape=(
            pltpu.VMEM((mine, width), BF16),
            pltpu.VMEM((tokens, hidden), BF16),
            pltpu.VMEM((hidden, width), BF16),
        ),
        in_specs=[anywhere] * 6,
        out_specs=(pl.BlockSpec(memory_space=pltpu.VMEM),) * 3,
        scratch_shapes=[
            pltpu.SMEM(block_mask.shape[1:], jnp.int32),
            pltpu.VMEM((hidden, width), BF16),
            pltpu.VMEM((tokens, hidden), BF16),
            pltpu.VMEM((tokens, hidden), BF16),
            pltpu.VMEM((mine, width), BF16),
            pltpu.VMEM((mine, width), BF16),
            pltpu.VMEM((2, tokens, half), F32),
            pltpu.VMEM((2, tokens, half), BF16),
            pltpu.VMEM((2, 2, reach, rows, half), BF16),
            pltpu.VMEM((2, 2, reach - 1, rows, half), BF16),
            pltpu.VMEM((2, n, mine, half), BF16),
            pltpu.VMEM((2, tokens, half), BF16),
            pltpu.VMEM((2, n, mine, half), BF16),
            pltpu.VMEM((2, n, mine, half), BF16),
            pltpu.VMEM((2, n, mine, half), F32),
            pltpu.VMEM((tokens, hidden), F32),
            pltpu.VMEM((2, hidden, tokens), BF16),
            pltpu.VMEM((2, tokens, hidden), F32),
            dma((4 + 2 * SUBS,)),
            dma((2, SUBS, 2, reach)),
            dma((3,)),
            dma((2, SUBS, 2, reach)),
            dma((2,)),
            dma((2,)),
            dma((2,)),
            dma((5,)),
            pltpu.SemaphoreType.REGULAR,
        ],
        compiler_params=pltpu.CompilerParams(collective_id=0, has_side_effects=True),
    )(stream_sent, grad_sent, preact_now, preact_back, down_weight, block_mask)
    return pl.pallas_call(
        store_kernel,
        name="store_outputs",
        out_shape=(
            jax.ShapeDtypeStruct(stream_sent.shape, BF16),
            jax.ShapeDtypeStruct(preact_back.shape, BF16),
            jax.ShapeDtypeStruct(down_weight.shape, BF16),
        ),
        in_specs=[pl.BlockSpec(memory_space=pltpu.VMEM)] * 3,
        out_specs=(anywhere,) * 3,
        scratch_shapes=[dma((3,))],
    )(*[pltpu.with_memory_space_constraint(a, pltpu.VMEM) for a in held])


def solution(mesh):
    n = math.isqrt(mesh.shape["blk"])
    placed = (
        P("section", "blk", None),
        P("section", "blk", None),
        P("section", None, "blk"),
        P("section", None, "blk"),
        P("section", "blk", None),
        P("section", "blk", None),
    )
    return jax.shard_map(
        functools.partial(body, n, mesh.shape["section"]),
        mesh=mesh,
        in_specs=placed,
        out_specs=(P("section", "blk", None), P("section", None, "blk"), P("section", "blk", None)),
        check_vma=False,
    )
```
